32 devices in a mesh: img: 4 (over z), sy: 2 (over x), sx: 4 (over y, core).
Axes of the slice: x: 2, y: 2, z: 4, core: 2. Of those that a mesh axis runs over, the one named last changes fastest.
Arguments:
- memory: bfloat16 [8, 20480, 256], P('img', ('sy', 'sx')), may hold values from -6 to 6
- enc_weight: bfloat16 [256, 256], replicated, may hold values from -0.375 to 0.375
- enc_bias: float32 [256], replicated, may hold values from -4 to 4
- norm_gain: float32 [256], replicated, may hold values from 0.25 to 1.75
- norm_bias: float32 [256], replicated, may hold values from -3 to 3
- class_weight: bfloat16 [256, 91], replicated, may hold values from -0.375 to 0.375
- class_bias: float32 [91], replicated, may hold values from -4 to 4
- box_w1: bfloat16 [256, 256], replicated, may hold values from -0.375 to 0.375
- box_b1: float32 [256], replicated, may hold values from -3 to 3
- box_w2: bfloat16 [256, 256], replicated, may hold values from -0.375 to 0.375
- box_b2: float32 [256], replicated, may hold values from -3 to 3
- box_w3: bfloat16 [256, 4], replicated, may hold values from -0.375 to 0.375
- box_b3: float32 [4], replicated, may hold values from -3 to 3
- picked: int32 [8, 320], P('img', ('sy', 'sx')), may hold values from 0 to 2559, as said below
- counts: int32 [8, 8], P('img', ('sy', 'sx')), may hold values from 1 to 40, 80 in all within a row
Outputs:
- token_logits: bfloat16 [8, 91, 20480], P('img', None, ('sy', 'sx'))
- token_boxes: float32 [8, 4, 20480], P('img', None, ('sy', 'sx'))
- query_feat: bfloat16 [8, 80, 256], P(None, 'img')
- query_logits: bfloat16 [8, 80, 91], P(None, 'img')
- query_boxes: bfloat16 [8, 80, 4], P(None, 'img')
The draws below stay inside these ranges and needn't reach their ends.
Inputs may be any that keep to these rules, and one draw needn't show every extreme that they name: `picked`: each tile's 40 entries are distinct local token indices in rising order; only the first counts of them are selected. Each image's counts sum to 80.
All inputs are finite; a program needn't handle non-finite values. No bound on the sum of `counts` on one device may be relied on, other than what follows from the above.
Results may differ from the reference program's by a relative error of at most 0.0041.
Values may be sent and summed in bfloat16 or wider, within the bound.
A program may use at most 64 MiB of HBM per device.

```python
import math
import jax
import jax.numpy as jnp
import numpy as np
from jax import lax

D = 256
CLS = 91
TILE_H = 40
TILE_W = 64
TOK_DEV = 2560
SHARDS = 8
B = 8
TOKENS = 20480
QUERIES = 80
MOST = 40
N_SY = 2
N_SX = 4


def draw_picked(key, part):
    keys = jax.random.split(jax.random.fold_in(key, 7), B * SHARDS)

    def subset(single):
        return jnp.sort(jax.random.permutation(single, TOK_DEV)[:MOST])
    chosen = jax.vmap(subset)(keys)
    return chosen.reshape(B, SHARDS * MOST).astype(jnp.int32)


def level_of(key, dims, cuts, least, high):
    def one(position, shards_of):
        steps = jax.random.uniform(jax.random.fold_in(jax.random.fold_in(key, 6), position), (shards_of,), jnp.float32, least / len(cuts), high / len(cuts))
        return jnp.repeat(jnp.exp(steps), dims[position] // shards_of).reshape((-1,) + (1,) * (len(dims) - position - 1))

    loudness = one(*cuts[0])
    for cut in cuts[1:]:
        loudness = loudness * one(*cut)
    return loudness


def length_profile(count, total, most, lean):
    portions = [(1 << 20) // math.isqrt(rank ** lean) + 1 for rank in range(2, count + 1)]
    rest, given = total - most - (count - 1), [1] * (count - 1)
    while rest > 0:
        movable = [i for i in range(count - 1) if given[i] < most]
        whole, left = sum([portions[i] for i in movable]), rest
        for i in movable:
            addition = min(most - given[i], max(1, left * portions[i] // whole), rest)
            given[i] = given[i] + addition
            rest = rest - addition
    return np.array([most] + given)


def uneven(own_key, number_of, total, reach, skew):
    if number_of == 2:
        one = jax.random.randint(own_key, (), max(1, total - reach), min(reach, total - 1) + 1)
        return jnp.stack([one, total - one])
    sizes = jnp.asarray(length_profile(number_of, total, reach, skew), jnp.int32)
    couples = (number_of - 1) // 2
    donor, taker = sizes[1:1 + 2 * couples:2], sizes[2:2 + 2 * couples:2]
    slack = jnp.minimum(donor - 1, reach - taker)
    moved = jax.random.randint(jax.random.fold_in(own_key, 1), (couples,), 0, 1 << 20) % (slack + 1)
    sizes = sizes.at[1:1 + 2 * couples:2].set(donor - moved).at[2:2 + 2 * couples:2].set(taker + moved)
    return sizes[jax.random.permutation(jax.random.fold_in(own_key, 2), number_of)]


def noise(key, extent, width, bound, cuts=(), kind=jnp.bfloat16):
    loudness = level_of(key, extent, cuts, -0.22, 0.18) if cuts else 1.0
    drawn = jax.random.normal(key, extent, jnp.float32) * width * loudness
    return jnp.minimum(jnp.maximum(drawn, -bound), bound).astype(kind)


def setup_inputs(seed: int = 0) -> dict:
    streams_of = jax.random.split(jax.random.key(seed), 16)
    return {
        "memory": noise(streams_of[0], (B, TOKENS, D), 1.0, 6.0, ((0, 4), (1, 8))),
        "enc_weight": noise(streams_of[1], (D, D), D ** -0.5, 0.375),
        "enc_bias": noise(streams_of[2], (D,), 1.0, 4.0, (), jnp.float32),
        "norm_gain": jnp.clip(1.0 + 0.15 * jax.random.normal(streams_of[3], (D,), jnp.float32), 0.25, 1.75),
        "norm_bias": noise(streams_of[4], (D,), 0.5, 3.0, (), jnp.float32),
        "class_weight": noise(streams_of[5], (D, CLS), D ** -0.5, 0.375),
        "class_bias": noise(streams_of[6], (CLS,), 1.0, 4.0, (), jnp.float32),
        "box_w1": noise(streams_of[7], (D, D), D ** -0.5, 0.375),
        "box_b1": noise(streams_of[8], (D,), 0.5, 3.0, (), jnp.float32),
        "box_w2": noise(streams_of[9], (D, D), D ** -0.5, 0.375),
        "box_b2": noise(streams_of[10], (D,), 0.5, 3.0, (), jnp.float32),
        "box_w3": noise(streams_of[11], (D, 4), D ** -0.5, 0.375),
        "box_b3": noise(streams_of[12], (4,), 0.5, 3.0, (), jnp.float32),
        "picked": draw_picked(jax.random.fold_in(streams_of[15], 71), 0),
        "counts": jax.vmap(lambda own: uneven(own, SHARDS, QUERIES, MOST, 2))(jax.random.split(streams_of[14], B)).reshape((B, SHARDS)).astype(jnp.int32),
    }


def reference(memory, enc_weight, enc_bias, norm_gain, norm_bias, class_weight, class_bias, box_w1, box_b1, box_w2, box_b2, box_w3, box_b3, picked, counts):
    index = jnp.arange(TOKENS).astype(jnp.int32)
    tile = index // TOK_DEV
    local = index % TOK_DEV
    row = tile // N_SX * TILE_H + local // TILE_W
    col = tile % N_SX * TILE_W + local % TILE_W
    center_x = (col.astype(jnp.float32) + 0.5) / (TILE_W * N_SX)
    center_y = (row.astype(jnp.float32) + 0.5) / (TILE_H * N_SY)
    sizes_wh = jnp.full((TOKENS,), 0.05, jnp.float32)
    prior = jnp.stack([center_x, center_y, sizes_wh, sizes_wh])
    prior_logit = jnp.log(prior / (1.0 - prior))

    def heads(mem):
        pre = jnp.dot(mem, enc_weight, preferred_element_type=jnp.float32) + enc_bias
        mean = lax.optimization_barrier(jnp.mean(pre, axis=-1, keepdims=True))
        centered = pre - mean
        var = lax.optimization_barrier(jnp.mean(centered * centered, axis=-1, keepdims=True))
        out_mem = (centered * lax.rsqrt(var + 1e-05) * norm_gain + norm_bias).astype(jnp.bfloat16)
        logits = (jnp.dot(out_mem, class_weight, preferred_element_type=jnp.float32) + class_bias).astype(jnp.bfloat16).T
        hidden = jax.nn.relu(jnp.dot(out_mem, box_w1, preferred_element_type=jnp.float32) + box_b1).astype(jnp.bfloat16)
        hidden = jax.nn.relu(jnp.dot(hidden, box_w2, preferred_element_type=jnp.float32) + box_b2).astype(jnp.bfloat16)
        delta = jnp.dot(hidden, box_w3, preferred_element_type=jnp.float32) + box_b3
        boxes = jax.nn.sigmoid(delta.T + prior_logit)
        return (out_mem, logits, boxes)
    out_mem, token_logits, token_boxes = lax.map(heads, memory)

    def choose(out_one, logit_one, box_one, pick_one, count_one):
        starts = jnp.cumsum(count_one) - count_one
        steps = jnp.arange(MOST).astype(jnp.int32)
        slot = starts[:, None] + steps[None, :]
        valid = steps[None, :] < count_one[:, None]
        slot = jnp.where(valid, slot, QUERIES).astype(jnp.int32)
        token = (jnp.arange(SHARDS).astype(jnp.int32) * TOK_DEV)[:, None] + pick_one.reshape(SHARDS, MOST)
        chosen = jnp.zeros((QUERIES,), jnp.int32).at[slot.reshape(-1)].set(token.reshape(-1).astype(jnp.int32), mode='drop')
        return (out_one[chosen], logit_one[:, chosen].T, box_one[:, chosen].T.astype(jnp.bfloat16))
    query_feat, query_logits, query_boxes = jax.vmap(choose)(out_mem, token_logits, token_boxes, picked, counts)
    return (token_logits, token_boxes, query_feat, query_logits, query_boxes)
```

```python
import functools
import jax
import jax.numpy as jnp
from jax import lax
from jax.experimental import pallas as pl
from jax.experimental.pallas import tpu as pltpu
from jax.sharding import PartitionSpec as P

TILE_H = 40
TILE_W = 64
Q_DEV = 20
MESH = pl.DeviceIdType.MESH
F32 = jnp.float32
BF = jnp.bfloat16


def up(n, m):
    return (n + m - 1) // m * m


def dot(a, b):
    return jnp.dot(a, b, preferred_element_type=F32)


def pad_lanes(x, lanes):
    if x.shape[1] == lanes:
        return x
    return jnp.concatenate([x, jnp.zeros((x.shape[0], lanes - x.shape[1]), x.dtype)], axis=1)


def transposed(ref):
    x = ref[...].astype(F32)
    return pad_lanes(x, up(x.shape[1], 128)).T.astype(BF)


def column(ref):
    x = pad_lanes(ref[...], up(ref.shape[1], 128))
    return jnp.broadcast_to(x, (128, x.shape[1])).T


def wide(col, lanes):
    return jnp.concatenate([col] * (lanes // 128), axis=1)


def prior_logit(center_x, center_y, k):
    prior = jnp.where(k == 0, center_x, jnp.where(k == 1, center_y, 0.05))
    return jnp.log(prior / (1.0 - prior))


def kernel(
    cfg,
    mem_hbm, we, be, ng, nb, wc, bc, w1, b1, w2, b2, w3, b3, picked, counts,
    logits_out, boxes_out, qf_out, ql_out, qb_out,
    mem_v, logits_v, boxes_v, wet, w1ct, w2t, w3t, bet, ngt, nbt, b1t, b2t, bct, b3t,
    sel, recv1, block, recv2,
    mem_sem, out_sem, send1, got1, send2, got2,
):
    n_img, n_sy, n_sx, chunk = cfg
    n = n_sy * n_sx
    images, tok, width = mem_v.shape
    cls = wc.shape[1]
    most = picked.shape[1]
    rows = sel.shape[1]
    g, sy, sx = lax.axis_index("img"), lax.axis_index("sy"), lax.axis_index("sx")
    tile = sy * n_sx + sx
    map_h, map_w = TILE_H * n_sy, TILE_W * n_sx
    my_i, my_q = tile // n_img, tile % n_img

    def at(img, t):
        return (img, t // n_sx, t % n_sx)

    loads = [pltpu.make_async_copy(mem_hbm.at[i], mem_v.at[i], mem_sem.at[i]) for i in range(images)]
    for load in loads:
        load.start()

    barrier = pltpu.get_barrier_semaphore()
    for off in range(1, n):
        pl.semaphore_signal(barrier, inc=1, device_id=at(g, (tile + off) % n), device_id_type=MESH)
    for off in range(1, n_img):
        for i in range(images):
            pl.semaphore_signal(
                barrier, inc=1, device_id=at((g + off) % n_img, i * n_img + g), device_id_type=MESH
            )

    wet[...] = transposed(we)
    w1ct[:width] = transposed(w1)
    w1ct[width:] = transposed(wc)[: w1ct.shape[0] - width]
    w2t[...] = transposed(w2)
    w3t[...] = transposed(w3)[: w3t.shape[0]]
    bet[...] = column(be)
    ngt[...] = column(ng)
    nbt[...] = column(nb)
    b1t[...] = column(b1)
    b2t[...] = column(b2)
    bct[...] = column(bc)
    b3t[...] = column(b3)[: b3t.shape[0]]

    diag = lax.broadcasted_iota(jnp.int32, (rows, most), 0) == lax.broadcasted_iota(jnp.int32, (rows, most), 1)
    spread = lax.broadcasted_iota(jnp.int32, (rows, tok), 1).astype(F32)
    real = lax.broadcasted_iota(jnp.int32, (rows, 1), 0) < most
    ids, mems = [], []
    for i in range(images):
        row = picked[i : i + 1, :].astype(F32)
        idx = jnp.sum(jnp.where(diag, row, 0.0), axis=1, keepdims=True)
        hot = jnp.where((spread == idx) & real, 1.0, 0.0).astype(BF)
        loads[i].wait()
        mems.append(dot(hot, mem_v[i]).astype(BF))
        ids.append(idx)
    mem_s = jnp.concatenate(mems, axis=0)
    idx = jnp.concatenate(ids, axis=0)
    pre = dot(mem_s, we[...]) + be[...]
    cen = pre - jnp.mean(pre, axis=1, keepdims=True)
    var = jnp.mean(cen * cen, axis=1, keepdims=True)
    out = (cen * lax.rsqrt(var + 1e-05) * ng[...] + nb[...]).astype(BF)
    cl = dot(out, pad_lanes(wc[...].astype(F32), 128).astype(BF)) + pad_lanes(bc[...], 128)
    hid = jnp.maximum(dot(out, w1[...]) + b1[...], 0.0).astype(BF)
    hid = jnp.maximum(dot(hid, w2[...]) + b2[...], 0.0).astype(BF)
    delta = dot(hid, pad_lanes(w3[...].astype(F32), 128).astype(BF)) + pad_lanes(b3[...], 128)
    at_row = jnp.floor((idx + 0.5) * (1.0 / TILE_W))
    at_col = idx - at_row * TILE_W
    cx = (at_col + (sx * TILE_W).astype(F32) + 0.5) / map_w
    cy = (at_row + (sy * TILE_H).astype(F32) + 0.5) / map_h
    lane = lax.broadcasted_iota(jnp.int32, delta.shape, 1)
    bx = pltpu.roll(jax.nn.sigmoid(delta + prior_logit(cx, cy, lane)), cls, 1)
    many = jnp.concatenate(
        [jnp.broadcast_to(counts[i : i + 1, :].astype(F32), (rows, 128)) for i in range(images)], axis=0
    )
    tail = jnp.where(lane < cls, cl, jnp.where(lane < cls + 4, bx, many)).astype(BF)
    for i in range(images):
        sel[i, :, :width] = out[i * rows : (i + 1) * rows]
        sel[i, :, width:] = tail[i * rows : (i + 1) * rows]

    pl.semaphore_wait(barrier, n - 1 + jnp.where(my_q == g, 0, n))

    sent = []
    for off in range(1, n):
        to = (tile + off) % n
        copy = pltpu.make_async_remote_copy(
            src_ref=sel.at[to // n_img], dst_ref=recv1.at[tile],
            send_sem=send1.at[off], recv_sem=got1.at[tile],
            device_id=at(g, to), device_id_type=MESH,
        )
        copy.start()
        sent.append(copy)
    own = pltpu.make_async_copy(sel.at[my_i], recv1.at[tile], got1.at[tile])
    own.start()

    def heads(i, first, count):
        def step(c, carry):
            lo = pl.multiple_of(c * chunk, 128)
            cols = pl.ds(lo, chunk)
            m = mem_v[i, cols, :]
            pre = lax.dot_general(wet[...], m, (((1,), (1,)), ((), ())), preferred_element_type=F32)
            pre = pre + wide(bet[...], chunk)
            cen = pre - jnp.mean(pre, axis=0, keepdims=True)
            var = jnp.mean(cen * cen, axis=0, keepdims=True)
            out = (cen * lax.rsqrt(var + 1e-05) * wide(ngt[...], chunk) + wide(nbt[...], chunk)).astype(BF)
            both = dot(w1ct[...], out)
            h = jnp.maximum(both[:width] + wide(b1t[...], chunk), 0.0).astype(BF)
            lg = both[width : width + cls] + wide(bct[:cls], chunk)
            logits_v[i, :, cols] = lg.astype(BF)
            h = jnp.maximum(dot(w2t[...], h) + wide(b2t[...], chunk), 0.0).astype(BF)
            delta = (dot(w3t[...], h) + wide(b3t[...], chunk))[:8]
            local = lo + lax.broadcasted_iota(jnp.int32, (8, chunk), 1)
            at_row = local // TILE_W
            at_col = local - at_row * TILE_W
            cx = ((at_col + sx * TILE_W).astype(F32) + 0.5) / map_w
            cy = ((at_row + sy * TILE_H).astype(F32) + 0.5) / map_h
            k = lax.broadcasted_iota(jnp.int32, (8, chunk), 0)
            boxes_v[i, :, cols] = jax.nn.sigmoid(delta + prior_logit(cx, cy, k))[:4]
            return carry

        lax.fori_loop(first, first + count, step, 0)

    outs = []

    def put(i):
        for a, b, s in ((logits_v, logits_out, 0), (boxes_v, boxes_out, 1)):
            copy = pltpu.make_async_copy(a.at[i], b.at[i], out_sem.at[i, s])
            copy.start()
            outs.append(copy)

    for i in range(images - 1):
        heads(i, 0, tok // chunk)
        put(i)

    own.wait()
    for off in range(1, n):
        frm = (tile + off) % n
        pltpu.make_async_remote_copy(
            src_ref=sel.at[0], dst_ref=recv1.at[frm], send_sem=send1.at[off], recv_sem=got1.at[frm],
            device_id=at(g, frm), device_id_type=MESH,
        ).wait_recv()
    start = (jnp.zeros((1, 1), F32) - (my_q * Q_DEV).astype(F32))
    k = lax.broadcasted_iota(jnp.int32, (rows, 128), 0).astype(F32)
    lane = lax.broadcasted_iota(jnp.int32, (rows, 128), 1).astype(F32)
    hots = []
    for s in range(n):
        have = recv1[s, :, width:].astype(F32)[0:1, cls + 4 : cls + 5]
        hots.append(jnp.where((k + start == lane) & (k < have), 1.0, 0.0))
        start = start + have
    hot = jnp.concatenate(hots, axis=0).T[: block.shape[0]].astype(BF)
    block[...] = dot(hot, recv1[...].reshape(n * rows, width + 128)).astype(BF)

    def hand(off):
        to = (tile + off) % n
        return pltpu.make_async_remote_copy(
            src_ref=block, dst_ref=recv2.at[g, my_i], send_sem=send2.at[off], recv_sem=got2.at[g, my_i],
            device_id=at(my_q, to), device_id_type=MESH,
        )

    for off in range(1, n):
        hand(off).start()

    @pl.when(my_q == g)
    def _():
        pltpu.make_async_copy(block, recv2.at[g, my_i], got2.at[g, my_i]).start()

    @pl.when(my_q != g)
    def _():
        hand(0).start()

    heads(images - 1, 0, tok // chunk)
    put(images - 1)

    for a in range(n_img):
        for i in range(images):
            pltpu.make_async_copy(block, recv2.at[a, i], got2.at[a, i]).wait()
            b = a * images + i
            qf_out[b] = recv2[a, i, :, :width][:Q_DEV]
            t = recv2[a, i, :, width:]
            ql_out[b] = t[:Q_DEV, :cls]
            qb_out[b] = pltpu.roll(t.astype(F32), 128 - cls, 1)[:Q_DEV, :4].astype(BF)

    for copy in sent:
        copy.wait_send()
    for off in range(1, n):
        hand(off).wait_send()

    @pl.when(my_q != g)
    def _():
        hand(0).wait_send()

    for copy in outs:
        copy.wait()


def shards(cfg, memory, we, be, ng, nb, wc, bc, w1, b1, w2, b2, w3, b3, picked, counts):
    n_img, n_sy, n_sx, chunk = cfg
    n = n_sy * n_sx
    images, tok, width = memory.shape
    cls = wc.shape[1]
    rows, qrows = up(picked.shape[1], 16), up(Q_DEV, 16)
    if images * n_img != n or cls + 5 > 128:
        raise ValueError("unsupported shape")
    total = images * n_img
    vm = pl.BlockSpec(memory_space=pltpu.VMEM)
    hbm = pl.BlockSpec(memory_space=pl.ANY)
    cpad = up(cls, 16)
    return pl.pallas_call(
        functools.partial(kernel, cfg),
        out_shape=(
            jax.ShapeDtypeStruct((images, cls, tok), BF),
            jax.ShapeDtypeStruct((images, 4, tok), F32),
            jax.ShapeDtypeStruct((total, Q_DEV, width), BF),
            jax.ShapeDtypeStruct((total, Q_DEV, cls), BF),
            jax.ShapeDtypeStruct((total, Q_DEV, 4), BF),
        ),
        in_specs=[hbm] + [vm] * 14,
        out_specs=(hbm, hbm, vm, vm, vm),
        scratch_shapes=[
            pltpu.VMEM((images, tok, width), BF),
            pltpu.VMEM((images, cls, tok), BF),
            pltpu.VMEM((images, 4, tok), F32),
            pltpu.VMEM((width, width), BF),
            pltpu.VMEM((width + cpad, width), BF),
            pltpu.VMEM((width, width), BF),
            pltpu.VMEM((16, width), BF),
            pltpu.VMEM((width, 128), F32),
            pltpu.VMEM((width, 128), F32),
            pltpu.VMEM((width, 128), F32),
            pltpu.VMEM((width, 128), F32),
            pltpu.VMEM((width, 128), F32),
            pltpu.VMEM((128, 128), F32),
            pltpu.VMEM((16, 128), F32),
            pltpu.VMEM((images, rows, width + 128), BF),
            pltpu.VMEM((n, rows, width + 128), BF),
            pltpu.VMEM((qrows, width + 128), BF),
            pltpu.VMEM((n_img, images, qrows, width + 128), BF),
            pltpu.SemaphoreType.DMA((images,)),
            pltpu.SemaphoreType.DMA((images, 2)),
            pltpu.SemaphoreType.DMA((n,)),
            pltpu.SemaphoreType.DMA((n,)),
            pltpu.SemaphoreType.DMA((n,)),
            pltpu.SemaphoreType.DMA((n_img, images)),
        ],
        compiler_params=pltpu.CompilerParams(collective_id=0, has_side_effects=True),
    )(
        memory, we, be[None], ng[None], nb[None], wc, bc[None], w1, b1[None], w2, b2[None], w3, b3[None],
        picked, counts,
    )


def solution(mesh):
    cfg = (mesh.shape["img"], mesh.shape["sy"], mesh.shape["sx"], 512)
    return jax.shard_map(
        functools.partial(shards, cfg),
        mesh=mesh,
        in_specs=(P("img", ("sy", "sx"), None),) + (P(),) * 12 + (P("img", ("sy", "sx")),) * 2,
        out_specs=(
            P("img", None, ("sy", "sx")),
            P("img", None, ("sy", "sx")),
            P(None, "img", None),
            P(None, "img", None),
            P(None, "img", None),
        ),
        check_vma=False,
    )
```

```python
import functools
import jax
import jax.numpy as jnp
from jax import lax
from jax.experimental import pallas as pl
from jax.experimental.pallas import tpu as pltpu
from jax.sharding import PartitionSpec as P

TILE_H = 40
TILE_W = 64
Q_DEV = 20
MESH = pl.DeviceIdType.MESH
F32 = jnp.float32
BF = jnp.bfloat16


def up(n, m):
    return (n + m - 1) // m * m


def dot(a, b):
    return jnp.dot(a, b, preferred_element_type=F32)


def dot_nt(a, b):
    return lax.dot_general(a, b, (((1,), (1,)), ((), ())), preferred_element_type=F32)


def pad_lanes(x, lanes):
    if x.shape[1] == lanes:
        return x
    return jnp.concatenate([x, jnp.zeros((x.shape[0], lanes - x.shape[1]), x.dtype)], axis=1)


def transposed(ref):
    x = ref[...].astype(F32)
    return pad_lanes(x, up(x.shape[1], 128)).T.astype(BF)


def column(ref):
    x = pad_lanes(ref[...], up(ref.shape[1], 128))
    return jnp.broadcast_to(x, (128, x.shape[1])).T


def pad_rows(x, rows):
    if x.shape[0] == rows:
        return x
    return jnp.concatenate([x, jnp.zeros((rows - x.shape[0], x.shape[1]), x.dtype)], axis=0)


def prepare(we, be, ng, nb, wct, bc, w1, b1, w2, b2, w3t, b3, images, prep):
    p_we, p_wc, p_w1, p_w2, p_w3, p_be, p_ng, p_nb, p_b1, p_b2, p_bc, p_b3 = prep
    cls, width = wct.shape
    p_we[...] = transposed(we)
    p_w1[...] = transposed(w1)
    p_w2[...] = transposed(w2)
    p_w3[...] = pad_rows(w3t[...].astype(F32), 16).astype(BF)
    xr = p_wc.shape[0]
    r = lax.broadcasted_iota(jnp.int32, (xr, 128), 0)
    c = lax.broadcasted_iota(jnp.int32, (xr, 128), 1)
    wpad = pad_rows(wct[...].astype(F32), 128).astype(BF)
    for i in range(images):
        pick = jnp.where(r == c * images + i, 1.0, 0.0).astype(BF)
        p_wc[:, i * width : (i + 1) * width] = dot(pick, wpad).astype(BF)
    mine = (r >= c * images) & (r < (c + 1) * images)
    p_bc[...] = jnp.broadcast_to(
        jnp.sum(jnp.where(mine, pad_lanes(bc[...], 128), 0.0), axis=1, keepdims=True), (xr, 128)
    )
    for p, v in ((p_be, be), (p_ng, ng), (p_nb, nb), (p_b1, b1), (p_b2, b2)):
        p[...] = column(v)
    p_b3[...] = column(b3)[: p_b3.shape[0]]


def prep_shapes(images, cls, width):
    xr = up(images * cls, 16)
    return [
        pltpu.VMEM((width, width), BF),
        pltpu.VMEM((xr, images * width), BF),
        pltpu.VMEM((width, width), BF),
        pltpu.VMEM((width, width), BF),
        pltpu.VMEM((16, width), BF),
    ] + [pltpu.VMEM((width, 128), F32)] * 5 + [pltpu.VMEM((xr, 128), F32), pltpu.VMEM((16, 128), F32)]


def heads(prep, mem_v, logits_v, boxes_v, lo, at_lo, chunk, place):
    p_we, p_wc, p_w1, p_w2, p_w3, p_be, p_ng, p_nb, p_b1, p_b2, p_bc, p_b3 = prep
    images, cls = mem_v.shape[0], logits_v.shape[0]
    sy, sx, map_h, map_w, first = place
    cols = pl.ds(at_lo, chunk)
    local = first + lo + lax.broadcasted_iota(jnp.int32, (8, chunk), 1)
    at_row = local // TILE_W
    at_col = local - at_row * TILE_W
    cx = ((at_col + sx * TILE_W).astype(F32) + 0.5) / map_w
    cy = ((at_row + sy * TILE_H).astype(F32) + 0.5) / map_h
    prior = prior_logit(cx, cy, lax.broadcasted_iota(jnp.int32, (8, chunk), 0))
    out_all = []
    for i in range(images):
        m = mem_v[i, pl.ds(lo, chunk), :]
        pre = lax.dot_general(p_we[...], m, (((1,), (1,)), ((), ())), preferred_element_type=F32)
        pre = pre + wide(p_be[...], chunk)
        cen = pre - jnp.mean(pre, axis=0, keepdims=True)
        var = jnp.mean(cen * cen, axis=0, keepdims=True)
        out = (cen * lax.rsqrt(var + 1e-05) * wide(p_ng[...], chunk) + wide(p_nb[...], chunk)).astype(BF)
        out_all.append(out)
        h = jnp.maximum(dot(p_w1[...], out) + wide(p_b1[...], chunk), 0.0).astype(BF)
        h = jnp.maximum(dot(p_w2[...], h) + wide(p_b2[...], chunk), 0.0).astype(BF)
        delta = (dot(p_w3[...], h) + wide(p_b3[...], chunk))[:8]
        boxes_v[i, :, cols] = jax.nn.sigmoid(delta + prior)[:4]
    lg = dot(p_wc[...], jnp.concatenate(out_all, axis=0)) + wide(p_bc[...], chunk)
    logits_v[:, :, cols] = lg.astype(BF)[: cls * images].reshape(cls, images, chunk)


def wide(col, lanes):
    return jnp.concatenate([col] * (lanes // 128), axis=1)


def prior_logit(center_x, center_y, k):
    prior = jnp.where(k == 0, center_x, jnp.where(k == 1, center_y, 0.05))
    return jnp.log(prior / (1.0 - prior))


def kernel(
    cfg,
    mem_hbm, we, be, ng, nb, wct, bc, w1, b1, w2, b2, w3t, b3, picked, counts,
    logits_v, boxes_v, qf_out, ql_out, qb_out,
    mem_v, sel, recv1, block, recv2, mem_sem, send1, got1, send2, got2,
    *prep,
):
    n_img, n_sy, n_sx, chunk, early, late = cfg
    n = n_sy * n_sx
    images, tok, width = mem_v.shape
    cls = wct.shape[0]
    most = picked.shape[1]
    rows = sel.shape[1]
    g, sy, sx = lax.axis_index("img"), lax.axis_index("sy"), lax.axis_index("sx")
    tile = sy * n_sx + sx
    map_h, map_w = TILE_H * n_sy, TILE_W * n_sx
    my_i, my_q = tile // n_img, tile % n_img

    def at(img, t):
        return (img, t // n_sx, t % n_sx)

    loads = [pltpu.make_async_copy(mem_hbm.at[i], mem_v.at[i], mem_sem.at[i]) for i in range(images)]
    for load in loads:
        load.start()

    barrier = pltpu.get_barrier_semaphore()
    for off in range(1, n):
        pl.semaphore_signal(barrier, inc=1, device_id=at(g, (tile + off) % n), device_id_type=MESH)
    for off in range(1, n_img):
        for i in range(images):
            pl.semaphore_signal(
                barrier, inc=1, device_id=at((g + off) % n_img, i * n_img + g), device_id_type=MESH
            )

    prepare(we, be, ng, nb, wct, bc, w1, b1, w2, b2, w3t, b3, images, prep)
    place = (sy, sx, map_h, map_w, 0)

    diag = lax.broadcasted_iota(jnp.int32, (rows, most), 0) == lax.broadcasted_iota(jnp.int32, (rows, most), 1)
    spread = lax.broadcasted_iota(jnp.int32, (rows, tok), 1).astype(F32)
    real = lax.broadcasted_iota(jnp.int32, (rows, 1), 0) < most
    ids, mems = [], []
    for i in range(images):
        row = picked[i : i + 1, :].astype(F32)
        idx = jnp.sum(jnp.where(diag, row, 0.0), axis=1, keepdims=True)
        hot = jnp.where((spread == idx) & real, 1.0, 0.0).astype(BF)
        loads[i].wait()
        mems.append(dot(hot, mem_v[i]).astype(BF))
        ids.append(idx)
    mem_s = jnp.concatenate(mems, axis=0)
    idx = jnp.concatenate(ids, axis=0)
    pre = dot(mem_s, we[...]) + be[...]
    cen = pre - jnp.mean(pre, axis=1, keepdims=True)
    var = jnp.mean(cen * cen, axis=1, keepdims=True)
    out = (cen * lax.rsqrt(var + 1e-05) * ng[...] + nb[...]).astype(BF)
    wpad = pad_rows(wct[...].astype(F32), 128).astype(BF)
    cl = dot_nt(out, wpad) + pad_lanes(bc[...], 128)
    hid = jnp.maximum(dot(out, w1[...]) + b1[...], 0.0).astype(BF)
    hid = jnp.maximum(dot(hid, w2[...]) + b2[...], 0.0).astype(BF)
    delta = dot_nt(hid, pad_rows(w3t[...].astype(F32), 128).astype(BF)) + pad_lanes(b3[...], 128)
    at_row = jnp.floor((idx + 0.5) * (1.0 / TILE_W))
    at_col = idx - at_row * TILE_W
    cx = (at_col + (sx * TILE_W).astype(F32) + 0.5) / map_w
    cy = (at_row + (sy * TILE_H).astype(F32) + 0.5) / map_h
    lane = lax.broadcasted_iota(jnp.int32, delta.shape, 1)
    bx = pltpu.roll(jax.nn.sigmoid(delta + prior_logit(cx, cy, lane)), cls, 1)
    many = jnp.concatenate(
        [jnp.broadcast_to(counts[:, i : i + 1].astype(F32), (rows, 128)) for i in range(images)], axis=0
    )
    tail = jnp.where(lane < cls, cl, jnp.where(lane < cls + 4, bx, many)).astype(BF)
    for i in range(images):
        sel[i, :, :width] = out[i * rows : (i + 1) * rows]
        sel[i, :, width:] = tail[i * rows : (i + 1) * rows]

    pl.semaphore_wait(barrier, n - 1 + jnp.where(my_q == g, 0, n))

    sent = []
    for off in range(1, n):
        to = (tile + off) % n
        copy = pltpu.make_async_remote_copy(
            src_ref=sel.at[to // n_img], dst_ref=recv1.at[tile],
            send_sem=send1.at[off], recv_sem=got1.at[tile],
            device_id=at(g, to), device_id_type=MESH,
        )
        copy.start()
        sent.append(copy)
    own = pltpu.make_async_copy(sel.at[my_i], recv1.at[tile], got1.at[tile])
    own.start()

    def some(first, count):
        def step(c, carry):
            lo = pl.multiple_of(c * chunk, 128)
            heads(prep, mem_v, logits_v, boxes_v, lo, lo, chunk, place)
            return carry

        lax.fori_loop(first, first + count, step, 0)

    some(0, early)

    own.wait()
    for off in range(1, n):
        frm = (tile + off) % n
        pltpu.make_async_remote_copy(
            src_ref=sel.at[0], dst_ref=recv1.at[frm], send_sem=send1.at[off], recv_sem=got1.at[frm],
            device_id=at(g, frm), device_id_type=MESH,
        ).wait_recv()
    start = (jnp.zeros((1, 1), F32) - (my_q * Q_DEV).astype(F32))
    k = lax.broadcasted_iota(jnp.int32, (rows, 128), 0).astype(F32)
    lane = lax.broadcasted_iota(jnp.int32, (rows, 128), 1).astype(F32)
    hots = []
    for s in range(n):
        have = recv1[s, :, width:].astype(F32)[0:1, cls + 4 : cls + 5]
        hots.append(jnp.where((k + start == lane) & (k < have), 1.0, 0.0))
        start = start + have
    hot = jnp.concatenate(hots, axis=0).T[: block.shape[0]].astype(BF)
    block[...] = dot(hot, recv1[...].reshape(n * rows, width + 128)).astype(BF)

    def hand(off):
        to = (tile + off) % n
        return pltpu.make_async_remote_copy(
            src_ref=block, dst_ref=recv2.at[g, my_i], send_sem=send2.at[off], recv_sem=got2.at[g, my_i],
            device_id=at(my_q, to), device_id_type=MESH,
        )

    for off in range(1, n):
        hand(off).start()

    @pl.when(my_q == g)
    def _():
        pltpu.make_async_copy(block, recv2.at[g, my_i], got2.at[g, my_i]).start()

    @pl.when(my_q != g)
    def _():
        hand(0).start()

    some(early, late)

    for a in range(n_img):
        for i in range(images):
            pltpu.make_async_copy(block, recv2.at[a, i], got2.at[a, i]).wait()
    total, qrows = n_img * images, block.shape[0]
    every = recv2[...].reshape(total * qrows, width + 128)
    r = lax.broadcasted_iota(jnp.int32, (Q_DEV * total, total * qrows), 0)
    c = lax.broadcasted_iota(jnp.int32, (Q_DEV * total, total * qrows), 1)
    turn = jnp.where(r % total * qrows + r // total == c, 1.0, 0.0).astype(BF)
    done = dot(turn, every).reshape(Q_DEV, total, width + 128)
    qf_out[...] = done[:, :, :width].astype(BF)
    ql_out[...] = done[:, :, width : width + cls].astype(BF)
    lane = lax.broadcasted_iota(jnp.int32, (16, 128), 1)
    k = lax.broadcasted_iota(jnp.int32, (16, 128), 0)
    which = jnp.where(lane == k + cls, 1.0, 0.0).astype(BF)
    for b in range(total):
        qb_out[b] = dot_nt(which, recv2[b // images, b % images, :, width:])[:4, :Q_DEV].astype(BF)

    for copy in sent:
        copy.wait_send()
    for off in range(1, n):
        hand(off).wait_send()

    @pl.when(my_q != g)
    def _():
        hand(0).wait_send()


def finish(
    cfg,
    mem_hbm, we, be, ng, nb, wct, bc, w1, b1, w2, b2, w3t, b3, logits_a, boxes_a, qf, ql, qb,
    logits_out, boxes_out, qf_out, ql_out, qb_out,
    mem_v, logits_v, boxes_v, mem_sem, out_sem,
    *prep,
):
    n_img, n_sy, n_sx, chunk, early, late = cfg
    images, rest, width = mem_v.shape
    done = (early + late) * chunk
    sy, sx = lax.axis_index("sy"), lax.axis_index("sx")
    load = pltpu.make_async_copy(mem_hbm.at[:, pl.ds(done, rest), :], mem_v, mem_sem)
    load.start()
    outs = [
        pltpu.make_async_copy(logits_a, logits_out.at[:, :, pl.ds(0, done)], out_sem.at[0]),
        pltpu.make_async_copy(boxes_a, boxes_out.at[:, :, pl.ds(0, done)], out_sem.at[1]),
    ]
    for copy in outs:
        copy.start()
    prepare(we, be, ng, nb, wct, bc, w1, b1, w2, b2, w3t, b3, images, prep)
    qf_out[...] = qf[...]
    ql_out[...] = ql[...]
    qb_out[...] = qb[...]
    load.wait()
    place = (sy, sx, TILE_H * n_sy, TILE_W * n_sx, done)

    def step(c, carry):
        lo = pl.multiple_of(c * chunk, 128)
        heads(prep, mem_v, logits_v, boxes_v, lo, lo, chunk, place)
        return carry

    lax.fori_loop(0, rest // chunk, step, 0)
    last = [
        pltpu.make_async_copy(logits_v, logits_out.at[:, :, pl.ds(done, rest)], out_sem.at[2]),
        pltpu.make_async_copy(boxes_v, boxes_out.at[:, :, pl.ds(done, rest)], out_sem.at[3]),
    ]
    for copy in last:
        copy.start()
    for copy in outs + last:
        copy.wait()


def shards(cfg, memory, we, be, ng, nb, wc, bc, w1, b1, w2, b2, w3, b3, picked, counts):
    n_img, n_sy, n_sx, chunk, early, late = cfg
    n = n_sy * n_sx
    images, tok, width = memory.shape
    cls = wc.shape[1]
    rows, qrows = up(picked.shape[1], 16), up(Q_DEV, 16)
    if images * n_img != n or cls + 5 > 128 or tok % chunk:
        raise ValueError("unsupported shape")
    total = images * n_img
    done = (early + late) * chunk
    vm = pl.BlockSpec(memory_space=pltpu.VMEM)
    hbm = pl.BlockSpec(memory_space=pl.ANY)
    weights = (we, be[None], ng[None], nb[None], wc.T, bc[None], w1, b1[None], w2, b2[None], w3.T, b3[None])

    def dense(count):
        return (jax.ShapeDtypeStruct((cls, images, count), BF), jax.ShapeDtypeStruct((images, 4, count), F32))

    slots = (
        jax.ShapeDtypeStruct((Q_DEV, total, width), BF),
        jax.ShapeDtypeStruct((Q_DEV, total, cls), BF),
        jax.ShapeDtypeStruct((total, 4, Q_DEV), BF),
    )
    first = pl.pallas_call(
        functools.partial(kernel, cfg),
        out_shape=dense(done) + slots,
        in_specs=[hbm] + [vm] * 14,
        out_specs=(vm,) * 5,
        scratch_shapes=[
            pltpu.VMEM((images, tok, width), BF),
            pltpu.VMEM((images, rows, width + 128), BF),
            pltpu.VMEM((n, rows, width + 128), BF),
            pltpu.VMEM((qrows, width + 128), BF),
            pltpu.VMEM((n_img, images, qrows, width + 128), BF),
            pltpu.SemaphoreType.DMA((images,)),
            pltpu.SemaphoreType.DMA((n,)),
            pltpu.SemaphoreType.DMA((n,)),
            pltpu.SemaphoreType.DMA((n,)),
            pltpu.SemaphoreType.DMA((n_img, images)),
        ] + prep_shapes(images, cls, width),
        compiler_params=pltpu.CompilerParams(collective_id=0, has_side_effects=True),
        name="exchange",
    )(memory, *weights, picked, counts.T)
    rest = tok - done
    logits, boxes, qf, ql, qb = pl.pallas_call(
        functools.partial(finish, cfg),
        out_shape=dense(tok) + slots,
        in_specs=[hbm] + [vm] * 17,
        out_specs=(hbm, hbm, vm, vm, vm),
        scratch_shapes=[
            pltpu.VMEM((images, rest, width), BF),
            pltpu.VMEM((cls, images, rest), BF),
            pltpu.VMEM((images, 4, rest), F32),
            pltpu.SemaphoreType.DMA,
            pltpu.SemaphoreType.DMA((4,)),
        ] + prep_shapes(images, cls, width),
        name="finish",
    )(memory, *weights, *first)
    return (
        jnp.transpose(logits, (1, 0, 2)), boxes, jnp.transpose(qf, (1, 0, 2)), jnp.transpose(ql, (1, 0, 2)),
        jnp.transpose(qb, (0, 2, 1)),
    )


def solution(mesh):
    cfg = (mesh.shape["img"], mesh.shape["sy"], mesh.shape["sx"], 256, 2, 3)
    return jax.shard_map(
        functools.partial(shards, cfg),
        mesh=mesh,
        in_specs=(P("img", ("sy", "sx"), None),) + (P(),) * 12 + (P("img", ("sy", "sx")),) * 2,
        out_specs=(
            P("img", None, ("sy", "sx")),
            P("img", None, ("sy", "sx")),
            P(None, "img", None),
            P(None, "img", None),
            P(None, "img", None),
        ),
        check_vma=False,
    )
```
